32 devices in a mesh: groups: 2 (over x), ctx: 16 (over z, y, core).
Axes of the slice: x: 2, y: 2, z: 4, core: 2. Of those that a mesh axis runs over, the one named last changes fastest.
Arguments:
- gate_short: bfloat16 [4096, 4096], P(('groups', 'ctx')), parts along dimension 0, may hold values from -6 to 6
- key_short: bfloat16 [4096, 4096], P(('groups', 'ctx')), parts along dimension 0, may hold values from -6 to 6
- value_short: bfloat16 [4096, 4096], P(('groups', 'ctx')), parts along dimension 0, may hold values from -6 to 6
- gate_long: bfloat16 [4096, 4096], P(('groups', 'ctx')), parts along dimension 0, may hold values from -6 to 6
- doc_ids: int32 [4096], P(('groups', 'ctx')), parts along dimension 0, may hold values from 0 to 7, never falling along the last dimension, each value on 1 to 512 neighbouring positions
- se_filter: float32 [7, 256], replicated, may hold values from -2 to 2
- long_filter: bfloat16 [256, 512], replicated, may hold values from -1.25 to 1.25
Outputs:
- scored: bfloat16 [4096, 4096], P(('groups', 'ctx')), parts along dimension 0
The draws below stay inside these ranges and needn't reach their ends.
There are 2 independent parts, one for each index of `groups`. The reference program is written for one: setup_inputs(seed, part) draws one part's arguments, and reference() takes and returns one part's arrays. A program takes and returns all parts, laid end to end along the dimension named above; an argument that names none is the same for every part. Nothing has to cross between parts.
Inputs may be any that keep to these rules, and one draw needn't show every extreme that they name: doc_ids never falls along the rows of a group; each document holds 1 to 512 consecutive rows, and one holds exactly 512.
All inputs are finite; a program needn't handle non-finite values.
Results may differ from the reference program's by a relative error of at most 0.0057.
Values may be sent and summed in bfloat16 or wider, within the bound.
A program may use at most 192 MiB of HBM per device.

```python
import math
import jax
import jax.numpy as jnp
import numpy as np
from jax import lax

C = 4096
FGROUP = 16
SHORT_TAPS = 7
STRETCH = 128
MAXDOC = 512
FILTERS = 256
TOKENS = 2048
DOCS = 8


def draw_long_filter(key, part):
    key_noise = jax.random.fold_in(key, 11)
    key_decay = jax.random.fold_in(key, 12)
    lag_axis = jnp.arange(MAXDOC, dtype=jnp.float32)[None, :]
    noise_draw = jax.random.truncated_normal(key_noise, -3.0, 3.0, (FILTERS, MAXDOC), jnp.float32)
    log_lowest = jnp.log(12.0)
    log_highest = jnp.log(8.0 * MAXDOC)
    decay_length = jnp.exp(jax.random.uniform(key_decay, (FILTERS, 1), jnp.float32, log_lowest, log_highest))
    norm_scale = jnp.sqrt(2.0 / jnp.minimum(decay_length, 1.0 * MAXDOC))
    return (noise_draw * jnp.exp(-lag_axis / decay_length) * norm_scale).astype(jnp.bfloat16)


def steps_of(stream_key, extent, pieces, least, top_value):
    gain, own = 1.0, jax.random.fold_in(stream_key, 6)
    for axis_at, shards_of in pieces:
        heights = jnp.exp(jax.random.uniform(jax.random.fold_in(own, axis_at), (shards_of,), jnp.float32, least / len(pieces), top_value / len(pieces)))
        gain = gain * jnp.repeat(heights, extent[axis_at] // shards_of).reshape([-1 if axis == axis_at else 1 for axis in range(len(extent))])
    return gain


def split_up(count, total, most, lean):
    loads = [(1 << 20) // math.isqrt(grade ** lean) + 1 for grade in range(2, count + 1)]
    surplus, counts = total - most - (count - 1), [1] * (count - 1)
    while surplus > 0:
        free = [i for i in range(count - 1) if counts[i] < most]
        mass, remaining = sum([loads[i] for i in free]), surplus
        for i in free:
            extra = min(most - counts[i], max(1, remaining * loads[i] // mass), surplus)
            counts[i] = counts[i] + extra
            surplus = surplus - extra
    return np.array([most] + counts)


def ragged_sizes(own_key, number_of, total, limit, skew):
    if number_of == 2:
        one = jax.random.randint(own_key, (), max(1, total - limit), min(limit, total - 1) + 1)
        return jnp.stack([one, total - one])
    sizes = jnp.asarray(split_up(number_of, total, limit, skew), jnp.int32)
    couples = (number_of - 1) // 2
    source_of, sink = sizes[1:1 + 2 * couples:2], sizes[2:2 + 2 * couples:2]
    slack = jnp.minimum(source_of - 1, limit - sink)
    moved = jax.random.randint(jax.random.fold_in(own_key, 1), (couples,), 0, 1 << 20) % (slack + 1)
    sizes = sizes.at[1:1 + 2 * couples:2].set(source_of - moved).at[2:2 + 2 * couples:2].set(sink + moved)
    return sizes[jax.random.permutation(jax.random.fold_in(own_key, 2), number_of)]


def gaussian(rng, extent, deviation, bound, cuts=(), kind=jnp.bfloat16):
    entries = deviation * jax.random.normal(rng, extent, jnp.float32)
    if cuts:
        entries = entries * steps_of(rng, extent, cuts, -0.22, 0.18)
    return jnp.clip(entries, -bound, bound).astype(kind)


def setup_inputs(seed: int = 0, part: int = 0) -> dict:
    seeds = jax.random.split(jax.random.key(seed), 8)
    part_splits = jax.random.split(jax.random.fold_in(seeds[7], part), 8)
    gate_short = gaussian(part_splits[0], (TOKENS, C), 1.0, 6.0, ((0, 16),))
    key_short = gaussian(part_splits[1], (TOKENS, C), 1.0, 6.0, ((0, 16),))
    value_short = gaussian(part_splits[2], (TOKENS, C), 1.0, 6.0, ((0, 16),))
    gate_long = gaussian(part_splits[3], (TOKENS, C), 1.0, 6.0, ((0, 16),))
    doc_ids = jnp.searchsorted(jnp.cumsum(ragged_sizes(part_splits[4], DOCS, TOKENS, MAXDOC, 2)), jnp.arange(TOKENS), side="right").astype(jnp.int32)
    se_filter = gaussian(seeds[5], (SHORT_TAPS, FILTERS), SHORT_TAPS ** -0.5, 2.0, (), jnp.float32)
    long_filter = draw_long_filter(jax.random.fold_in(seeds[7], 71), part)
    return dict(gate_short=gate_short, key_short=key_short, value_short=value_short, gate_long=gate_long, doc_ids=doc_ids, se_filter=se_filter, long_filter=long_filter)


def short_mixing(key_value, doc_ids, se_filter):
    row_count = key_value.shape[0]
    widened = jnp.repeat(se_filter, FGROUP, axis=1)
    values = key_value.astype(jnp.float32)
    summed = jnp.zeros(values.shape, jnp.float32)
    for tap_index in range(SHORT_TAPS):
        shifted = jnp.concatenate([jnp.zeros((tap_index, values.shape[1]), jnp.float32), values], 0)[:row_count]
        shifted_doc = jnp.concatenate([jnp.full((tap_index,), -1, jnp.int32), doc_ids], 0)[:row_count]
        agreeing = (shifted_doc == doc_ids).astype(jnp.float32)
        summed = summed + widened[tap_index][None, :] * agreeing[:, None] * shifted
    return summed


def long_mixing(mixed, doc_ids, long_filter):
    row_count, chan_count = mixed.shape
    filter_count = long_filter.shape[0]
    window = (MAXDOC // STRETCH + 1) * STRETCH
    front_rows = window - STRETCH
    padded = jnp.concatenate([jnp.zeros((front_rows, chan_count), mixed.dtype), mixed], 0)
    padded_doc = jnp.concatenate([jnp.full((front_rows,), -1, jnp.int32), doc_ids], 0)
    target_pos = lax.broadcasted_iota(jnp.int32, (STRETCH, window), 0)
    source_pos = lax.broadcasted_iota(jnp.int32, (STRETCH, window), 1)
    lag_table = target_pos + front_rows - source_pos
    inside = (lag_table >= 0) & (lag_table < MAXDOC)
    filter_taps = jnp.take(long_filter.astype(jnp.float32), jnp.clip(lag_table, 0, MAXDOC - 1), axis=1)
    filter_taps = jnp.where(inside[None], filter_taps, jnp.zeros_like(filter_taps))

    def one_tile(tile_index):
        begin_row = (tile_index * STRETCH).astype(jnp.int32)
        rows_win = lax.dynamic_slice_in_dim(padded, begin_row, window, 0).astype(jnp.float32)
        docs_win = lax.dynamic_slice_in_dim(padded_doc, begin_row, window, 0)
        docs_tgt = lax.dynamic_slice_in_dim(doc_ids, begin_row, STRETCH, 0)
        agreeing = (docs_tgt[:, None] == docs_win[None, :]).astype(jnp.float32)
        weights = filter_taps * agreeing[None]
        result = jnp.einsum("gtp,pgk->tgk", weights, rows_win.reshape(window, filter_count, -1))
        return result.reshape(STRETCH, chan_count)

    tile_results = lax.map(one_tile, jnp.arange(row_count // STRETCH, dtype=jnp.int32))
    return tile_results.reshape(row_count, chan_count)


def reference(gate_short, key_short, value_short, gate_long, doc_ids, se_filter, long_filter):
    key_value = (key_short.astype(jnp.float32) * value_short.astype(jnp.float32)).astype(jnp.bfloat16)
    key_value = lax.optimization_barrier(key_value)
    short_mix = short_mixing(key_value, doc_ids, se_filter)
    mixed = (gate_short.astype(jnp.float32) * short_mix).astype(jnp.bfloat16)
    mixed = lax.optimization_barrier(mixed)
    long_mix = long_mixing(mixed, doc_ids, long_filter)
    return (gate_long.astype(jnp.float32) * long_mix).astype(jnp.bfloat16)
```

```python
import functools

import jax
import jax.numpy as jnp
from jax import lax
from jax.experimental import pallas as pl
from jax.experimental.pallas import tpu as pltpu
from jax.sharding import PartitionSpec as P

MAXDOC = 512
REACH = 4
RIM = 16
LANES = 128
CHUNKS = 8
MESH = pl.DeviceIdType.MESH


def kernel(
    count, gs_ref, k_ref, v_ref, gl_ref, doc_ref, se_ref, h_ref, out_ref,
    own, own_doc, rim_out, rim_in, got, got_doc, taps, rev, near_w, acc, agree, far_mask, near_mask,
    send_sem, recv_sem, doc_send, doc_recv, rim_send, rim_recv,
):
    rows, chans = gs_ref.shape
    tap_count = se_ref.shape[0]
    filters = h_ref.shape[0]
    width = chans // CHUNKS
    tiles = width // LANES
    fgroup = chans // filters
    per_tile = LANES // fgroup
    half = rows // 2
    span = MAXDOC + rows
    f32, bf16 = jnp.float32, jnp.bfloat16

    me = lax.axis_index("ctx")
    at = lax.rem(me, REACH)
    core = lax.rem(me, 2)
    upper = at // 2
    core_mate = me + 1 - 2 * core
    row_mate = me + 2 - 4 * upper
    has_prev = me >= REACH
    has_next = me + REACH < count
    is_first = me == 0
    is_last = me == count - 1

    barrier = pltpu.get_barrier_semaphore()

    def greet(target):
        pl.semaphore_signal(barrier, inc=1, device_id={"ctx": target}, device_id_type=MESH)

    greet(core_mate)
    greet(row_mate)
    pl.when(has_prev)(lambda: greet(me - REACH))
    pl.when(has_next)(lambda: greet(me + REACH))
    pl.when(me > 0)(lambda: greet(me - 1))
    pl.when(me < count - 1)(lambda: greet(me + 1))

    doc_row = jnp.broadcast_to(doc_ref[...].astype(f32), (rows, rows))
    doc_col = doc_row.T
    near_mask[...] = (doc_row == doc_col).astype(f32)
    own_doc[...] = doc_col.astype(bf16)
    kv_tail = k_ref[rows - RIM :, :].astype(f32) * v_ref[rows - RIM :, :].astype(f32)
    rim_out[:, :chans] = kv_tail.astype(bf16)
    rim_out[:, chans:] = doc_col[rows - RIM :, :].astype(bf16)

    peers = 2 + has_prev.astype(jnp.int32) + has_next.astype(jnp.int32)
    peers = peers + (me > 0).astype(jnp.int32) + (me < count - 1).astype(jnp.int32)
    pl.semaphore_wait(barrier, peers)

    def remote(src, dst, ssem, rsem, target):
        return pltpu.make_async_remote_copy(
            src_ref=src, dst_ref=dst, send_sem=ssem, recv_sem=rsem,
            device_id={"ctx": target}, device_id_type=MESH,
        )

    def rim_copy(target):
        return remote(rim_out, rim_in, rim_send, rim_recv, target)

    pl.when(me < count - 1)(lambda: rim_copy(me + 1).start())

    def block_copy(slot, j, src, target):
        return remote(src, got.at[slot, j], send_sem.at[slot, j], recv_sem.at[slot, j], target)

    def doc_copy(slot, src, target):
        return remote(src, got_doc.at[slot], doc_send.at[slot], doc_recv.at[slot], target)

    def start(slot, j, source, target):
        block, docs = (own.at[j], own_doc) if source is None else (got.at[source, j], got_doc.at[source])
        pl.when(j == 0)(lambda: doc_copy(slot, docs, target).start())
        block_copy(slot, j, block, target).start()

    def await_recv(slot, j):
        pl.when(j == 0)(lambda: doc_copy(slot, own_doc, core_mate).wait_recv())
        block_copy(slot, j, own.at[j], core_mate).wait_recv()

    def await_send(slot, j):
        pl.when(j == 0)(lambda: doc_copy(slot, own_doc, core_mate).wait_send())
        block_copy(slot, j, own.at[j], core_mate).wait_send()

    @pl.when(jnp.logical_not(has_prev))
    def _():
        got[0] = jnp.zeros(got.shape[1:], bf16)
        got_doc[0] = jnp.full(got_doc.shape[1:], -1.0, bf16)

    @pl.when(is_first)
    def _():
        rim_in[:, :chans] = jnp.zeros((RIM, chans), bf16)
        rim_in[:, chans:] = jnp.full((RIM, LANES), -1.0, bf16)

    for piece in range(span // LANES):
        lag = lax.broadcasted_iota(jnp.int32, (MAXDOC, LANES), 0)
        pos = lax.broadcasted_iota(jnp.int32, (MAXDOC, LANES), 1) + piece * LANES
        flip = jnp.where(lag + pos == MAXDOC, 1.0, 0.0).astype(bf16)
        rev[:, piece * LANES : (piece + 1) * LANES] = jnp.dot(
            h_ref[...], flip, preferred_element_type=f32
        )

    @pl.when(me > 0)
    def _():
        rim_copy(core_mate).wait_recv()

    doc_ext = jnp.concatenate([rim_in[:, chans:].astype(f32), doc_col], 0)
    for tap in range(tap_count):
        agree[tap] = (doc_ext[RIM - tap : RIM - tap + rows] == doc_col).astype(f32)

    def short_chunk(j, _):
        for tile in range(tiles):
            lanes = pl.ds(pl.multiple_of(j * width + tile * LANES, LANES), LANES)
            kv = (k_ref[:, lanes].astype(f32) * v_ref[:, lanes].astype(f32)).astype(bf16).astype(f32)
            ext = jnp.concatenate([rim_in[:, lanes].astype(f32), kv], 0)
            weights = se_ref[:, lanes]
            total = kv * weights[0:1, :]
            for tap in range(1, tap_count):
                shifted = ext[RIM - tap : RIM - tap + rows]
                total = total + (shifted * agree[tap]) * weights[tap : tap + 1, :]
            mixed = gs_ref[:, lanes].astype(f32) * total
            own[j, :, tile * LANES : (tile + 1) * LANES] = mixed.astype(bf16)
        pl.when(has_next)(lambda: start(0, j, None, me + REACH))
        pl.when(upper == 0)(lambda: start(2, j, None, row_mate))
        pl.when(core == 0)(lambda: start(1, j, None, core_mate))
        return 0

    lax.fori_loop(0, CHUNKS, short_chunk, 0)

    lane_group = lax.broadcasted_iota(jnp.int32, (1, LANES), 1) // fgroup

    def pick(result, height, lanes):
        picked = result[0:height, lanes]
        for g in range(1, per_tile):
            picked = jnp.where(lane_group == g, result[g * height : (g + 1) * height, lanes], picked)
        return picked

    def prepare(j, tile):
        ct = j * tiles + tile
        first = pl.multiple_of(ct * per_tile, per_tile)
        filt = rev[pl.ds(first, per_tile), :]
        for g in range(per_tile):
            line = filt[g : g + 1, :]
            low = pltpu.roll(jnp.broadcast_to(line, (half, span)), 0, 1, stride=1, stride_axis=0)
            tail = line[:, span - 2 * LANES :]
            high = pltpu.roll(jnp.broadcast_to(tail, (half, 2 * LANES)), half, 1, stride=1, stride_axis=0)
            base = pl.multiple_of((ct * per_tile + g) * half, half)
            taps[pl.ds(base, half), :] = low[:, :MAXDOC].astype(bf16)
            near_w[g * rows : g * rows + half, :] = (low[:, MAXDOC:] * near_mask[:half, :]).astype(bf16)
            near_w[g * rows + half : (g + 1) * rows, :] = (high[:, LANES:] * near_mask[half:, :]).astype(bf16)
        block = own[j, :, pl.ds(pl.multiple_of(tile * LANES, LANES), LANES)]
        result = jnp.dot(near_w[...], block, preferred_element_type=f32)
        acc[ct] = pick(result, rows, slice(0, LANES))

    leader = jnp.broadcast_to(doc_row[0:1, 0:1], (rows, LANES))
    near_mask_out = (doc_col == leader).astype(f32)
    agree[0] = near_mask_out

    def far(j, tile):
        ct = j * tiles + tile
        lanes = pl.ds(pl.multiple_of(tile * LANES, LANES), LANES)
        pieces = []
        for w in range(REACH):
            q = lax.rem(at + w, REACH)
            slot = (q // 2 + at // 2) % 2 * 2 + (q + at) % 2
            pieces.append(got[slot, j, :, lanes] * far_mask[w])
        left = jnp.concatenate(pieces, 0)
        right = jnp.concatenate([left[half:], jnp.zeros((half, LANES), bf16)], 0)
        base = pl.multiple_of(ct * per_tile * half, per_tile * half)
        result = jnp.dot(
            taps[pl.ds(base, per_tile * half), :],
            jnp.concatenate([left, right], 1),
            preferred_element_type=f32,
        )
        both = jnp.concatenate(
            [pick(result, half, slice(0, LANES)), pick(result, half, slice(LANES, 2 * LANES))], 0
        )
        total = acc[ct] + both * agree[0]
        wide = pl.ds(pl.multiple_of(ct * LANES, LANES), LANES)
        out_ref[:, wide] = (gl_ref[:, wide].astype(f32) * total).astype(bf16)

    def step(s, _):
        @pl.when(s < CHUNKS)
        def _():
            lax.fori_loop(0, tiles, lambda tile, c: (prepare(s, tile), c)[1], 0)
            pl.when(has_prev)(lambda: await_recv(0, s))
            pl.when(upper == 1)(lambda: start(2, s, 0, row_mate))
            pl.when(core == 1)(lambda: start(1, s, 0, core_mate))

        @pl.when((s >= 1) & (s < CHUNKS + 1))
        def _():
            await_recv(2, s - 1)
            start(3, s - 1, 2, core_mate)

        @pl.when(s >= 2)
        def _():
            j = s - 2
            await_recv(1, j)
            await_recv(3, j)

            @pl.when(j == 0)
            def _():
                for w in range(REACH):
                    q = lax.rem(at + w, REACH)
                    slot = (q // 2 + at // 2) % 2 * 2 + (q + at) % 2
                    far_mask[w] = (got_doc[slot].astype(f32) == leader).astype(bf16)

            lax.fori_loop(0, tiles, lambda tile, c: (far(j, tile), c)[1], 0)

        return 0

    lax.fori_loop(0, CHUNKS + 2, step, 0)

    def drain(j, _):
        pl.when(has_next)(lambda: await_send(0, j))
        for slot in (1, 2, 3):
            await_send(slot, j)
        return 0

    lax.fori_loop(0, CHUNKS, drain, 0)
    pl.when(me < count - 1)(lambda: rim_copy(core_mate).wait_send())


def body(gate_short, key_short, value_short, gate_long, doc_ids, se_filter, long_filter):
    rows, chans = gate_short.shape
    tap_count, filters = se_filter.shape
    fgroup = chans // filters
    count = lax.axis_size("ctx")
    assert rows * REACH == MAXDOC and rows == LANES and count % REACH == 0
    width = chans // CHUNKS
    bf16, f32 = jnp.bfloat16, jnp.float32
    widened = jnp.repeat(se_filter, fgroup, axis=1)
    vmem = pl.BlockSpec(memory_space=pltpu.VMEM)
    return pl.pallas_call(
        functools.partial(kernel, count),
        out_shape=jax.ShapeDtypeStruct((rows, chans), bf16),
        in_specs=[vmem] * 7,
        out_specs=vmem,
        scratch_shapes=[
            pltpu.VMEM((CHUNKS, rows, width), bf16),
            pltpu.VMEM((rows, LANES), bf16),
            pltpu.VMEM((RIM, chans + LANES), bf16),
            pltpu.VMEM((RIM, chans + LANES), bf16),
            pltpu.VMEM((REACH, CHUNKS, rows, width), bf16),
            pltpu.VMEM((REACH, rows, LANES), bf16),
            pltpu.VMEM((filters * rows // 2, MAXDOC), bf16),
            pltpu.VMEM((filters, MAXDOC + rows), f32),
            pltpu.VMEM((LANES // fgroup * rows, rows), bf16),
            pltpu.VMEM((chans // LANES, rows, LANES), f32),
            pltpu.VMEM((tap_count, rows, LANES), f32),
            pltpu.VMEM((REACH, rows, LANES), bf16),
            pltpu.VMEM((rows, rows), f32),
            pltpu.SemaphoreType.DMA((REACH, CHUNKS)),
            pltpu.SemaphoreType.DMA((REACH, CHUNKS)),
            pltpu.SemaphoreType.DMA((REACH,)),
            pltpu.SemaphoreType.DMA((REACH,)),
            pltpu.SemaphoreType.DMA,
            pltpu.SemaphoreType.DMA,
        ],
        compiler_params=pltpu.CompilerParams(
            collective_id=0, has_side_effects=True, vmem_limit_bytes=56 * 1024 * 1024
        ),
    )(gate_short, key_short, value_short, gate_long, doc_ids.reshape(1, rows), widened, long_filter)


def solution(mesh):
    placed = P(("groups", "ctx"), None)
    return jax.shard_map(
        body,
        mesh=mesh,
        in_specs=(placed, placed, placed, placed, P(("groups", "ctx")), P(), P()),
        out_specs=placed,
        check_vma=False,
    )
```

```python
import functools

import jax
import jax.numpy as jnp
from jax import lax
from jax.experimental import pallas as pl
from jax.experimental.pallas import tpu as pltpu
from jax.sharding import PartitionSpec as P

MAXDOC = 512
REACH = 4
RIM = 16
STEP = 16
LANES = 128
CHUNKS = 16
MESH = pl.DeviceIdType.MESH


def kernel(
    count, gs_ref, k_ref, v_ref, gl_ref, doc_ref, se_ref, h_ref, out_ref,
    own, own_doc, rim_out, rim_in, got, got_doc, taps, rev, near_w, acc, agree, far_mask, near_mask,
    send_sem, recv_sem, doc_send, doc_recv, rim_send, rim_recv,
):
    rows, chans = gs_ref.shape
    tap_count = se_ref.shape[0]
    filters = h_ref.shape[0]
    width = chans // CHUNKS
    tiles = width // LANES
    fgroup = chans // filters
    per_tile = LANES // fgroup
    half = rows // 2
    span = MAXDOC + rows
    f32, bf16 = jnp.float32, jnp.bfloat16

    me = lax.axis_index("ctx")
    at = lax.rem(me, REACH)
    core = lax.rem(me, 2)
    upper = at // 2
    core_mate = me + 1 - 2 * core
    row_mate = me + 2 - 4 * upper
    has_prev = me >= REACH
    has_next = me + REACH < count
    is_first = me == 0
    is_last = me == count - 1

    barrier = pltpu.get_barrier_semaphore()

    def greet(target):
        pl.semaphore_signal(barrier, inc=1, device_id={"ctx": target}, device_id_type=MESH)

    greet(core_mate)
    greet(row_mate)
    pl.when(has_prev)(lambda: greet(me - REACH))
    pl.when(has_next)(lambda: greet(me + REACH))
    pl.when(me > 0)(lambda: greet(me - 1))
    pl.when(me < count - 1)(lambda: greet(me + 1))

    doc_row = jnp.broadcast_to(doc_ref[...].astype(f32), (rows, rows))
    doc_col = doc_row.T
    near_mask[...] = (doc_row == doc_col).astype(bf16)
    own_doc[...] = doc_col.astype(bf16)
    kv_tail = k_ref[rows - RIM :, :].astype(f32) * v_ref[rows - RIM :, :].astype(f32)
    rim_out[:, :chans] = kv_tail.astype(bf16)
    rim_out[:, chans:] = doc_col[rows - RIM :, :].astype(bf16)

    peers = 2 + has_prev.astype(jnp.int32) + has_next.astype(jnp.int32)
    peers = peers + (me > 0).astype(jnp.int32) + (me < count - 1).astype(jnp.int32)
    pl.semaphore_wait(barrier, peers)

    def remote(src, dst, ssem, rsem, target):
        return pltpu.make_async_remote_copy(
            src_ref=src, dst_ref=dst, send_sem=ssem, recv_sem=rsem,
            device_id={"ctx": target}, device_id_type=MESH,
        )

    def rim_copy(target):
        return remote(rim_out, rim_in, rim_send, rim_recv, target)

    pl.when(me < count - 1)(lambda: rim_copy(me + 1).start())

    def block_copy(slot, j, src, target):
        return remote(src, got.at[slot, j], send_sem.at[slot, j], recv_sem.at[slot, j], target)

    def doc_copy(slot, src, target):
        return remote(src, got_doc.at[slot], doc_send.at[slot], doc_recv.at[slot], target)

    def start(slot, j, source, target):
        block, docs = (own.at[j], own_doc) if source is None else (got.at[source, j], got_doc.at[source])
        pl.when(j == 0)(lambda: doc_copy(slot, docs, target).start())
        block_copy(slot, j, block, target).start()

    def await_recv(slot, j):
        pl.when(j == 0)(lambda: doc_copy(slot, own_doc, core_mate).wait_recv())
        block_copy(slot, j, own.at[j], core_mate).wait_recv()

    def await_send(slot, j):
        pl.when(j == 0)(lambda: doc_copy(slot, own_doc, core_mate).wait_send())
        block_copy(slot, j, own.at[j], core_mate).wait_send()

    @pl.when(is_first)
    def _():
        rim_in[:, :chans] = jnp.zeros((RIM, chans), bf16)
        rim_in[:, chans:] = jnp.full((RIM, LANES), -1.0, bf16)

    @pl.when(me > 0)
    def _():
        rim_copy(core_mate).wait_recv()

    doc_ext = jnp.concatenate([rim_in[:, chans:].astype(f32), doc_col], 0)
    for tap in range(tap_count):
        agree[tap] = (doc_ext[RIM - tap : RIM - tap + rows] == doc_col).astype(f32)

    def short_chunk(j, _):
        source = lax.broadcasted_iota(jnp.int32, (filters, width), 0)
        target = lax.broadcasted_iota(jnp.int32, (filters, width), 1) // fgroup
        spread = (source - j * (width // fgroup) == target).astype(f32)
        widened = jnp.dot(
            se_ref[...], spread, precision=lax.Precision.HIGHEST, preferred_element_type=f32
        )
        for tile in range(tiles):
            lanes = pl.ds(pl.multiple_of(j * width + tile * LANES, LANES), LANES)
            kv = (k_ref[:, lanes].astype(f32) * v_ref[:, lanes].astype(f32)).astype(bf16).astype(f32)
            ext = jnp.concatenate([rim_in[:, lanes].astype(f32), kv], 0)
            weights = widened[:, tile * LANES : (tile + 1) * LANES]
            total = kv * weights[0:1, :]
            for tap in range(1, tap_count):
                shifted = ext[RIM - tap : RIM - tap + rows]
                total = total + (shifted * agree[tap]) * weights[tap : tap + 1, :]
            mixed = gs_ref[:, lanes].astype(f32) * total
            own[j, :, tile * LANES : (tile + 1) * LANES] = mixed.astype(bf16)
        pl.when(has_next)(lambda: start(0, j, None, me + REACH))
        pl.when(upper == 0)(lambda: start(2, j, None, row_mate))
        pl.when(core == 0)(lambda: start(1, j, None, core_mate))
        return 0

    lax.fori_loop(0, CHUNKS, short_chunk, 0)

    @pl.when(jnp.logical_not(has_prev))
    def _():
        got[0] = jnp.zeros(got.shape[1:], bf16)
        got_doc[0] = jnp.full(got_doc.shape[1:], -1.0, bf16)

    for piece in range(span // LANES):
        lag = lax.broadcasted_iota(jnp.int32, (MAXDOC, LANES), 0)
        pos = lax.broadcasted_iota(jnp.int32, (MAXDOC, LANES), 1) + piece * LANES
        flip = jnp.where(lag + pos == MAXDOC, 1.0, 0.0).astype(bf16)
        rev[:, piece * LANES : (piece + 1) * LANES] = jnp.dot(
            h_ref[...], flip, preferred_element_type=f32
        )

    lane_group = lax.broadcasted_iota(jnp.int32, (1, LANES), 1) // fgroup

    def pick(result, height, lanes):
        picked = result[0:height, lanes]
        for g in range(1, per_tile):
            picked = jnp.where(lane_group == g, result[g * height : (g + 1) * height, lanes], picked)
        return picked

    def prepare(j, tile):
        ct = j * tiles + tile
        first = pl.multiple_of(ct * per_tile, per_tile)
        filt = rev[pl.ds(first, per_tile), :]
        for g in range(per_tile):
            line = jnp.broadcast_to(filt[g : g + 1, :], (STEP, span))
            base = pltpu.roll(line, 0, 1, stride=1, stride_axis=0).astype(bf16)
            tail = base[:, span - 2 * LANES :]
            for r in range(rows // STEP):
                low = slice(r * STEP, (r + 1) * STEP)
                if r * STEP < half:
                    turned = base if r == 0 else pltpu.roll(base, r * STEP, 1)
                    at_row = pl.multiple_of((ct * per_tile + g) * half + r * STEP, STEP)
                    taps[pl.ds(at_row, STEP), :] = turned[:, :MAXDOC]
                    near = turned[:, MAXDOC:]
                else:
                    near = pltpu.roll(tail, r * STEP, 1)[:, LANES:]
                near_w[g * rows + r * STEP : g * rows + (r + 1) * STEP, :] = near * near_mask[low, :]
        block = own[j, :, pl.ds(pl.multiple_of(tile * LANES, LANES), LANES)]
        result = jnp.dot(near_w[...], block, preferred_element_type=f32)
        acc[ct] = pick(result, rows, slice(0, LANES))

    leader = jnp.broadcast_to(doc_row[0:1, 0:1], (rows, LANES))
    near_mask_out = (doc_col == leader).astype(f32)
    agree[0] = near_mask_out

    def far(j, tile):
        ct = j * tiles + tile
        lanes = pl.ds(pl.multiple_of(tile * LANES, LANES), LANES)
        pieces = []
        for w in range(REACH):
            q = lax.rem(at + w, REACH)
            slot = (q // 2 + at // 2) % 2 * 2 + (q + at) % 2
            pieces.append(got[slot, j, :, lanes] * far_mask[w])
        left = jnp.concatenate(pieces, 0)
        right = jnp.concatenate([left[half:], jnp.zeros((half, LANES), bf16)], 0)
        base = pl.multiple_of(ct * per_tile * half, per_tile * half)
        result = jnp.dot(
            taps[pl.ds(base, per_tile * half), :],
            jnp.concatenate([left, right], 1),
            preferred_element_type=f32,
        )
        both = jnp.concatenate(
            [pick(result, half, slice(0, LANES)), pick(result, half, slice(LANES, 2 * LANES))], 0
        )
        total = acc[ct] + both * agree[0]
        wide = pl.ds(pl.multiple_of(ct * LANES, LANES), LANES)
        out_ref[:, wide] = (gl_ref[:, wide].astype(f32) * total).astype(bf16)

    def step(s, _):
        @pl.when(s < CHUNKS)
        def _():
            lax.fori_loop(0, tiles, lambda tile, c: (prepare(s, tile), c)[1], 0)
            pl.when(has_prev)(lambda: await_recv(0, s))
            pl.when(upper == 1)(lambda: start(2, s, 0, row_mate))
            pl.when(core == 1)(lambda: start(1, s, 0, core_mate))

        @pl.when((s >= 1) & (s < CHUNKS + 1))
        def _():
            await_recv(2, s - 1)
            start(3, s - 1, 2, core_mate)

        @pl.when(s >= 2)
        def _():
            j = s - 2
            await_recv(1, j)
            await_recv(3, j)

            @pl.when(j == 0)
            def _():
                for w in range(REACH):
                    q = lax.rem(at + w, REACH)
                    slot = (q // 2 + at // 2) % 2 * 2 + (q + at) % 2
                    far_mask[w] = (got_doc[slot].astype(f32) == leader).astype(bf16)

            lax.fori_loop(0, tiles, lambda tile, c: (far(j, tile), c)[1], 0)

        return 0

    lax.fori_loop(0, CHUNKS + 2, step, 0)

    def drain(j, _):
        pl.when(has_next)(lambda: await_send(0, j))
        for slot in (1, 2, 3):
            await_send(slot, j)
        return 0

    lax.fori_loop(0, CHUNKS, drain, 0)
    pl.when(me < count - 1)(lambda: rim_copy(core_mate).wait_send())


def body(gate_short, key_short, value_short, gate_long, doc_ids, se_filter, long_filter):
    rows, chans = gate_short.shape
    tap_count, filters = se_filter.shape
    fgroup = chans // filters
    count = lax.axis_size("ctx")
    assert rows * REACH == MAXDOC and rows == LANES and count % REACH == 0
    width = chans // CHUNKS
    bf16, f32 = jnp.bfloat16, jnp.float32
    vmem = pl.BlockSpec(memory_space=pltpu.VMEM)
    return pl.pallas_call(
        functools.partial(kernel, count),
        out_shape=jax.ShapeDtypeStruct((rows, chans), bf16),
        in_specs=[vmem] * 7,
        out_specs=vmem,
        scratch_shapes=[
            pltpu.VMEM((CHUNKS, rows, width), bf16),
            pltpu.VMEM((rows, LANES), bf16),
            pltpu.VMEM((RIM, chans + LANES), bf16),
            pltpu.VMEM((RIM, chans + LANES), bf16),
            pltpu.VMEM((REACH, CHUNKS, rows, width), bf16),
            pltpu.VMEM((REACH, rows, LANES), bf16),
            pltpu.VMEM((filters * rows // 2, MAXDOC), bf16),
            pltpu.VMEM((filters, MAXDOC + rows), f32),
            pltpu.VMEM((LANES // fgroup * rows, rows), bf16),
            pltpu.VMEM((chans // LANES, rows, LANES), f32),
            pltpu.VMEM((tap_count, rows, LANES), f32),
            pltpu.VMEM((REACH, rows, LANES), bf16),
            pltpu.VMEM((rows, rows), bf16),
            pltpu.SemaphoreType.DMA((REACH, CHUNKS)),
            pltpu.SemaphoreType.DMA((REACH, CHUNKS)),
            pltpu.SemaphoreType.DMA((REACH,)),
            pltpu.SemaphoreType.DMA((REACH,)),
            pltpu.SemaphoreType.DMA,
            pltpu.SemaphoreType.DMA,
        ],
        compiler_params=pltpu.CompilerParams(
            collective_id=0, has_side_effects=True, vmem_limit_bytes=56 * 1024 * 1024
        ),
    )(gate_short, key_short, value_short, gate_long, doc_ids.reshape(1, rows), se_filter, long_filter)


def solution(mesh):
    placed = P(("groups", "ctx"), None)
    return jax.shard_map(
        body,
        mesh=mesh,
        in_specs=(placed, placed, placed, placed, P(("groups", "ctx")), P(), P()),
        out_specs=placed,
        check_vma=False,
    )
```

```python
import functools

import jax
import jax.numpy as jnp
from jax import lax
from jax.experimental import pallas as pl
from jax.experimental.pallas import tpu as pltpu
from jax.sharding import PartitionSpec as P

MAXDOC = 512
REACH = 4
RIM = 16
STEP = 16
LANES = 128
CHUNKS = 16
MESH = pl.DeviceIdType.MESH


def kernel(
    count, gs_ref, k_ref, v_ref, gl_ref, doc_ref, se_ref, h_ref, out_ref,
    own, own_doc, rim_out, rim_in, got, got_doc, taps, rev, near_w, acc, agree, far_mask, near_mask,
    send_sem, recv_sem, doc_send, doc_recv, rim_send, rim_recv,
):
    rows, chans = gs_ref.shape
    tap_count = se_ref.shape[0]
    filters = h_ref.shape[0]
    width = chans // CHUNKS
    tiles = width // LANES
    fgroup = chans // filters
    per_tile = LANES // fgroup
    half = rows // 2
    packed = per_tile // 2
    span = MAXDOC + rows
    f32, bf16 = jnp.float32, jnp.bfloat16

    me = lax.axis_index("ctx")
    at = lax.rem(me, REACH)
    core = lax.rem(me, 2)
    upper = at // 2
    core_mate = me + 1 - 2 * core
    row_mate = me + 2 - 4 * upper
    has_prev = me >= REACH
    has_next = me + REACH < count
    is_first = me == 0
    is_last = me == count - 1

    barrier = pltpu.get_barrier_semaphore()

    def greet(target):
        pl.semaphore_signal(barrier, inc=1, device_id={"ctx": target}, device_id_type=MESH)

    greet(core_mate)
    greet(row_mate)
    pl.when(has_prev)(lambda: greet(me - REACH))
    pl.when(has_next)(lambda: greet(me + REACH))
    pl.when(me > 0)(lambda: greet(me - 1))
    pl.when(me < count - 1)(lambda: greet(me + 1))

    doc_row = jnp.broadcast_to(doc_ref[...].astype(f32), (rows, rows))
    doc_col = doc_row.T
    near_mask[...] = (doc_row == doc_col).astype(bf16)
    own_doc[...] = doc_col.astype(bf16)
    kv_tail = k_ref[rows - RIM :, :].astype(f32) * v_ref[rows - RIM :, :].astype(f32)
    rim_out[:, :chans] = kv_tail.astype(bf16)
    rim_out[:, chans:] = doc_col[rows - RIM :, :].astype(bf16)

    peers = 2 + has_prev.astype(jnp.int32) + has_next.astype(jnp.int32)
    peers = peers + (me > 0).astype(jnp.int32) + (me < count - 1).astype(jnp.int32)
    pl.semaphore_wait(barrier, peers)

    def remote(src, dst, ssem, rsem, target):
        return pltpu.make_async_remote_copy(
            src_ref=src, dst_ref=dst, send_sem=ssem, recv_sem=rsem,
            device_id={"ctx": target}, device_id_type=MESH,
        )

    def rim_copy(target):
        return remote(rim_out, rim_in, rim_send, rim_recv, target)

    pl.when(me < count - 1)(lambda: rim_copy(me + 1).start())

    def block_copy(slot, j, src, target):
        return remote(src, got.at[slot, j], send_sem.at[slot, j], recv_sem.at[slot, j], target)

    def doc_copy(slot, src, target):
        return remote(src, got_doc.at[slot], doc_send.at[slot], doc_recv.at[slot], target)

    def start(slot, j, source, target):
        block, docs = (own.at[j], own_doc) if source is None else (got.at[source, j], got_doc.at[source])
        pl.when(j == 0)(lambda: doc_copy(slot, docs, target).start())
        block_copy(slot, j, block, target).start()

    def await_recv(slot, j):
        pl.when(j == 0)(lambda: doc_copy(slot, own_doc, core_mate).wait_recv())
        block_copy(slot, j, own.at[j], core_mate).wait_recv()

    def await_send(slot, j):
        pl.when(j == 0)(lambda: doc_copy(slot, own_doc, core_mate).wait_send())
        block_copy(slot, j, own.at[j], core_mate).wait_send()

    @pl.when(is_first)
    def _():
        rim_in[:, :chans] = jnp.zeros((RIM, chans), bf16)
        rim_in[:, chans:] = jnp.full((RIM, LANES), -1.0, bf16)

    @pl.when(me > 0)
    def _():
        rim_copy(core_mate).wait_recv()

    doc_ext = jnp.concatenate([rim_in[:, chans:].astype(f32), doc_col], 0)
    for tap in range(tap_count):
        agree[tap] = (doc_ext[RIM - tap : RIM - tap + rows] == doc_col).astype(f32)

    left_over, terms = se_ref[...], []
    for _ in range(3):
        term = left_over.astype(bf16).astype(f32)
        left_over = left_over - term
        terms += [term, jnp.zeros((8 - tap_count, filters), f32)]
    se_parts = jnp.concatenate(terms, 0).astype(bf16)

    def short_chunk(j, _):
        source = lax.broadcasted_iota(jnp.int32, (filters, width), 0)
        target = lax.broadcasted_iota(jnp.int32, (filters, width), 1) // fgroup
        spread = jnp.where(source - j * (width // fgroup) == target, 1.0, 0.0).astype(bf16)
        parts = jnp.dot(se_parts, spread, preferred_element_type=f32)
        widened = parts[0:tap_count] + parts[8 : 8 + tap_count] + parts[16 : 16 + tap_count]
        for tile in range(tiles):
            lanes = pl.ds(pl.multiple_of(j * width + tile * LANES, LANES), LANES)
            kv = (k_ref[:, lanes].astype(f32) * v_ref[:, lanes].astype(f32)).astype(bf16).astype(f32)
            ext = jnp.concatenate([rim_in[:, lanes].astype(f32), kv], 0)
            weights = widened[:, tile * LANES : (tile + 1) * LANES]
            total = kv * weights[0:1, :]
            for tap in range(1, tap_count):
                shifted = ext[RIM - tap : RIM - tap + rows]
                total = total + (shifted * agree[tap]) * weights[tap : tap + 1, :]
            mixed = gs_ref[:, lanes].astype(f32) * total
            own[j, :, tile * LANES : (tile + 1) * LANES] = mixed.astype(bf16)
        pl.when(has_next)(lambda: start(0, j, None, me + REACH))
        pl.when(upper == 0)(lambda: start(2, j, None, row_mate))
        pl.when(core == 0)(lambda: start(1, j, None, core_mate))
        return 0

    lax.fori_loop(0, CHUNKS, short_chunk, 0)

    @pl.when(jnp.logical_not(has_prev))
    def _():
        got[0] = jnp.zeros(got.shape[1:], bf16)
        got_doc[0] = jnp.full(got_doc.shape[1:], -1.0, bf16)

    for piece in range(span // LANES):
        lag = lax.broadcasted_iota(jnp.int32, (MAXDOC, LANES), 0)
        pos = lax.broadcasted_iota(jnp.int32, (MAXDOC, LANES), 1) + piece * LANES
        flip = jnp.where(lag + pos == MAXDOC, 1.0, 0.0).astype(bf16)
        rev[:, piece * LANES : (piece + 1) * LANES] = jnp.dot(
            h_ref[...], flip, preferred_element_type=f32
        )

    lane_group = lax.broadcasted_iota(jnp.int32, (1, LANES), 1) // fgroup

    def pick(result, height, lanes):
        picked = result[0:height, lanes]
        for g in range(1, per_tile):
            picked = jnp.where(lane_group == g, result[g * height : (g + 1) * height, lanes], picked)
        return picked

    def prepare(j, tile):
        ct = j * tiles + tile
        first = pl.multiple_of(ct * per_tile, per_tile)
        filt = rev[pl.ds(first, per_tile), :]
        for g in range(per_tile):
            line = jnp.broadcast_to(filt[g : g + 1, :], (STEP, span))
            base = pltpu.roll(line, 0, 1, stride=1, stride_axis=0).astype(bf16)
            tail = base[:, span - 2 * LANES :]
            for r in range(rows // STEP):
                low = slice(r * STEP, (r + 1) * STEP)
                if r * STEP < half:
                    turned = base if r == 0 else pltpu.roll(base, r * STEP, 1)
                    at_row = pl.multiple_of((ct * per_tile + g) * half + r * STEP, STEP)
                    taps[pl.ds(at_row, STEP), :] = turned[:, :MAXDOC]
                    near = turned[:, MAXDOC:]
                else:
                    near = pltpu.roll(tail, r * STEP, 1)[:, LANES:]
                e, side = g % packed, g // packed
                near_w[tile, e * rows + r * STEP : e * rows + (r + 1) * STEP, side * rows : (side + 1) * rows] = (
                    near * near_mask[low, :]
                )
        block = own[j, :, tile * LANES : (tile + 1) * LANES]
        none = jnp.zeros_like(block)
        first_side = lax.broadcasted_iota(jnp.int32, (rows, LANES), 1) < LANES // 2
        block = jnp.concatenate([jnp.where(first_side, block, none), jnp.where(first_side, none, block)], 0)
        result = jnp.dot(near_w[tile], block, preferred_element_type=f32)
        picked = result[0:rows]
        for e in range(1, packed):
            picked = jnp.where(lane_group % packed == e, result[e * rows : (e + 1) * rows], picked)
        acc[ct] = picked

    leader = jnp.broadcast_to(doc_row[0:1, 0:1], (rows, LANES))
    near_mask_out = (doc_col == leader).astype(f32)
    agree[0] = near_mask_out

    def far(j, tile):
        ct = j * tiles + tile
        lanes = slice(tile * LANES, (tile + 1) * LANES)
        pieces = []
        for w in range(REACH):
            q = lax.rem(at + w, REACH)
            slot = (q // 2 + at // 2) % 2 * 2 + (q + at) % 2
            pieces.append(got[slot, j, :, lanes] * far_mask[w])
        left = jnp.concatenate(pieces, 0)
        right = jnp.concatenate([left[half:], jnp.zeros((half, LANES), bf16)], 0)
        base = pl.multiple_of(ct * per_tile * half, per_tile * half)
        result = jnp.dot(
            taps[pl.ds(base, per_tile * half), :],
            jnp.concatenate([left, right], 1),
            preferred_element_type=f32,
        )
        both = jnp.concatenate(
            [pick(result, half, slice(0, LANES)), pick(result, half, slice(LANES, 2 * LANES))], 0
        )
        total = acc[ct] + both * agree[0]
        wide = pl.ds(pl.multiple_of(ct * LANES, LANES), LANES)
        out_ref[:, wide] = (gl_ref[:, wide].astype(f32) * total).astype(bf16)

    def step(s, _):
        @pl.when(s < CHUNKS)
        def _():
            for tile in range(tiles):
                prepare(s, tile)
            pl.when(has_prev)(lambda: await_recv(0, s))
            pl.when(upper == 1)(lambda: start(2, s, 0, row_mate))
            pl.when(core == 1)(lambda: start(1, s, 0, core_mate))

        @pl.when((s >= 1) & (s < CHUNKS + 1))
        def _():
            await_recv(2, s - 1)
            start(3, s - 1, 2, core_mate)

        @pl.when(s >= 2)
        def _():
            j = s - 2
            await_recv(1, j)
            await_recv(3, j)

            @pl.when(j == 0)
            def _():
                for w in range(REACH):
                    q = lax.rem(at + w, REACH)
                    slot = (q // 2 + at // 2) % 2 * 2 + (q + at) % 2
                    far_mask[w] = (got_doc[slot].astype(f32) == leader).astype(bf16)

            for tile in range(tiles):
                far(j, tile)

        return 0

    lax.fori_loop(0, CHUNKS + 2, step, 0)

    def drain(j, _):
        pl.when(has_next)(lambda: await_send(0, j))
        for slot in (1, 2, 3):
            await_send(slot, j)
        return 0

    lax.fori_loop(0, CHUNKS, drain, 0)
    pl.when(me < count - 1)(lambda: rim_copy(core_mate).wait_send())


def body(gate_short, key_short, value_short, gate_long, doc_ids, se_filter, long_filter):
    rows, chans = gate_short.shape
    tap_count, filters = se_filter.shape
    fgroup = chans // filters
    count = lax.axis_size("ctx")
    assert rows * REACH == MAXDOC and rows == LANES and count % REACH == 0
    width = chans // CHUNKS
    bf16, f32 = jnp.bfloat16, jnp.float32
    vmem = pl.BlockSpec(memory_space=pltpu.VMEM)
    return pl.pallas_call(
        functools.partial(kernel, count),
        out_shape=jax.ShapeDtypeStruct((rows, chans), bf16),
        in_specs=[vmem] * 7,
        out_specs=vmem,
        scratch_shapes=[
            pltpu.VMEM((CHUNKS, rows, width), bf16),
            pltpu.VMEM((rows, LANES), bf16),
            pltpu.VMEM((RIM, chans + LANES), bf16),
            pltpu.VMEM((RIM, chans + LANES), bf16),
            pltpu.VMEM((REACH, CHUNKS, rows, width), bf16),
            pltpu.VMEM((REACH, rows, LANES), bf16),
            pltpu.VMEM((filters * rows // 2, MAXDOC), bf16),
            pltpu.VMEM((filters, MAXDOC + rows), f32),
            pltpu.VMEM((width // LANES, LANES // fgroup // 2 * rows, 2 * rows), bf16),
            pltpu.VMEM((chans // LANES, rows, LANES), f32),
            pltpu.VMEM((tap_count, rows, LANES), f32),
            pltpu.VMEM((REACH, rows, LANES), bf16),
            pltpu.VMEM((rows, rows), bf16),
            pltpu.SemaphoreType.DMA((REACH, CHUNKS)),
            pltpu.SemaphoreType.DMA((REACH, CHUNKS)),
            pltpu.SemaphoreType.DMA((REACH,)),
            pltpu.SemaphoreType.DMA((REACH,)),
            pltpu.SemaphoreType.DMA,
            pltpu.SemaphoreType.DMA,
        ],
        compiler_params=pltpu.CompilerParams(
            collective_id=0, has_side_effects=True, vmem_limit_bytes=56 * 1024 * 1024
        ),
    )(gate_short, key_short, value_short, gate_long, doc_ids.reshape(1, rows), se_filter, long_filter)


def solution(mesh):
    placed = P(("groups", "ctx"), None)
    return jax.shard_map(
        body,
        mesh=mesh,
        in_specs=(placed, placed, placed, placed, P(("groups", "ctx")), P(), P()),
        out_specs=placed,
        check_vma=False,
    )
```

```python
import functools

import jax
import jax.numpy as jnp
from jax import lax
from jax.experimental import pallas as pl
from jax.experimental.pallas import tpu as pltpu
from jax.sharding import PartitionSpec as P

MAXDOC = 512
REACH = 4
RIM = 16
STEP = 16
LANES = 128
CHUNKS = 16
MESH = pl.DeviceIdType.MESH


def kernel(
    count, gs_ref, k_ref, v_ref, gl_ref, doc_ref, se_ref, h_ref, out_ref,
    own, own_doc, rim_out, rim_in, got, got_doc, taps, rev, near_w, acc, agree, far_mask, near_mask,
    send_sem, recv_sem, doc_send, doc_recv, rim_send, rim_recv,
):
    rows, chans = gs_ref.shape
    tap_count = se_ref.shape[0]
    filters = h_ref.shape[0]
    width = chans // CHUNKS
    tiles = width // LANES
    fgroup = chans // filters
    per_tile = LANES // fgroup
    half = rows // 2
    span = MAXDOC + rows
    f32, bf16 = jnp.float32, jnp.bfloat16

    me = lax.axis_index("ctx")
    at = lax.rem(me, REACH)
    core = lax.rem(me, 2)
    upper = at // 2
    core_mate = me + 1 - 2 * core
    row_mate = me + 2 - 4 * upper
    has_prev = me >= REACH
    has_next = me + REACH < count
    is_first = me == 0
    is_last = me == count - 1

    barrier = pltpu.get_barrier_semaphore()

    def greet(target):
        pl.semaphore_signal(barrier, inc=1, device_id={"ctx": target}, device_id_type=MESH)

    greet(core_mate)
    greet(row_mate)
    pl.when(has_prev)(lambda: greet(me - REACH))
    pl.when(has_next)(lambda: greet(me + REACH))
    pl.when(me > 0)(lambda: greet(me - 1))
    pl.when(me < count - 1)(lambda: greet(me + 1))

    doc_row = jnp.broadcast_to(doc_ref[...].astype(f32), (rows, rows))
    doc_col = doc_row.T
    near_mask[...] = (doc_row == doc_col).astype(bf16)
    own_doc[...] = doc_col.astype(bf16)
    kv_tail = k_ref[rows - RIM :, :].astype(f32) * v_ref[rows - RIM :, :].astype(f32)
    rim_out[:, :chans] = kv_tail.astype(bf16)
    rim_out[:, chans:] = doc_col[rows - RIM :, :].astype(bf16)

    peers = 2 + has_prev.astype(jnp.int32) + has_next.astype(jnp.int32)
    peers = peers + (me > 0).astype(jnp.int32) + (me < count - 1).astype(jnp.int32)
    pl.semaphore_wait(barrier, peers)

    def remote(src, dst, ssem, rsem, target):
        return pltpu.make_async_remote_copy(
            src_ref=src, dst_ref=dst, send_sem=ssem, recv_sem=rsem,
            device_id={"ctx": target}, device_id_type=MESH,
        )

    def rim_copy(target):
        return remote(rim_out, rim_in, rim_send, rim_recv, target)

    pl.when(me < count - 1)(lambda: rim_copy(me + 1).start())

    def block_copy(slot, j, src, target):
        return remote(src, got.at[slot, j], send_sem.at[slot, j], recv_sem.at[slot, j], target)

    def doc_copy(slot, src, target):
        return remote(src, got_doc.at[slot], doc_send.at[slot], doc_recv.at[slot], target)

    def start(slot, j, source, target):
        block, docs = (own.at[j], own_doc) if source is None else (got.at[source, j], got_doc.at[source])
        pl.when(j == 0)(lambda: doc_copy(slot, docs, target).start())
        block_copy(slot, j, block, target).start()

    def await_recv(slot, j):
        pl.when(j == 0)(lambda: doc_copy(slot, own_doc, core_mate).wait_recv())
        block_copy(slot, j, own.at[j], core_mate).wait_recv()

    def await_send(slot, j):
        pl.when(j == 0)(lambda: doc_copy(slot, own_doc, core_mate).wait_send())
        block_copy(slot, j, own.at[j], core_mate).wait_send()

    @pl.when(is_first)
    def _():
        rim_in[:, :chans] = jnp.zeros((RIM, chans), bf16)
        rim_in[:, chans:] = jnp.full((RIM, LANES), -1.0, bf16)

    @pl.when(me > 0)
    def _():
        rim_copy(core_mate).wait_recv()

    doc_ext = jnp.concatenate([rim_in[:, chans:].astype(f32), doc_col], 0)
    for tap in range(tap_count):
        agree[tap] = (doc_ext[RIM - tap : RIM - tap + rows] == doc_col).astype(f32)

    left_over, terms = se_ref[...], []
    for _ in range(3):
        term = left_over.astype(bf16).astype(f32)
        left_over = left_over - term
        terms += [term, jnp.zeros((8 - tap_count, filters), f32)]
    se_parts = jnp.concatenate(terms, 0).astype(bf16)

    def short_chunk(j, _):
        source = lax.broadcasted_iota(jnp.int32, (filters, width), 0)
        target = lax.broadcasted_iota(jnp.int32, (filters, width), 1) // fgroup
        spread = jnp.where(source - j * (width // fgroup) == target, 1.0, 0.0).astype(bf16)
        parts = jnp.dot(se_parts, spread, preferred_element_type=f32)
        widened = parts[0:tap_count] + parts[8 : 8 + tap_count] + parts[16 : 16 + tap_count]
        for tile in range(tiles):
            lanes = pl.ds(pl.multiple_of(j * width + tile * LANES, LANES), LANES)
            kv = (k_ref[:, lanes].astype(f32) * v_ref[:, lanes].astype(f32)).astype(bf16).astype(f32)
            ext = jnp.concatenate([rim_in[:, lanes].astype(f32), kv], 0)
            weights = widened[:, tile * LANES : (tile + 1) * LANES]
            total = kv * weights[0:1, :]
            for tap in range(1, tap_count):
                shifted = ext[RIM - tap : RIM - tap + rows]
                total = total + (shifted * agree[tap]) * weights[tap : tap + 1, :]
            mixed = gs_ref[:, lanes].astype(f32) * total
            own[j, :, tile * LANES : (tile + 1) * LANES] = mixed.astype(bf16)
        pl.when(has_next)(lambda: start(0, j, None, me + REACH))
        pl.when(upper == 0)(lambda: start(2, j, None, row_mate))
        pl.when(core == 0)(lambda: start(1, j, None, core_mate))
        return 0

    lax.fori_loop(0, CHUNKS, short_chunk, 0)

    @pl.when(jnp.logical_not(has_prev))
    def _():
        got[0] = jnp.zeros(got.shape[1:], bf16)
        got_doc[0] = jnp.full(got_doc.shape[1:], -1.0, bf16)

    for piece in range(span // LANES):
        lag = lax.broadcasted_iota(jnp.int32, (MAXDOC, LANES), 0)
        pos = lax.broadcasted_iota(jnp.int32, (MAXDOC, LANES), 1) + piece * LANES
        flip = jnp.where(lag + pos == MAXDOC, 1.0, 0.0).astype(bf16)
        rev[:, piece * LANES : (piece + 1) * LANES] = jnp.dot(
            h_ref[...], flip, preferred_element_type=f32
        )

    lane_group = lax.broadcasted_iota(jnp.int32, (1, LANES), 1) // fgroup

    def pick(result, height, lanes):
        picked = result[0:height, lanes]
        for g in range(1, per_tile):
            picked = jnp.where(lane_group == g, result[g * height : (g + 1) * height, lanes], picked)
        return picked

    def prepare(j, tile):
        ct = j * tiles + tile
        first = pl.multiple_of(ct * per_tile, per_tile)
        filt = rev[pl.ds(first, per_tile), :]
        for g in range(per_tile):
            line = jnp.broadcast_to(filt[g : g + 1, :], (STEP, span))
            base = pltpu.roll(line, 0, 1, stride=1, stride_axis=0).astype(bf16)
            tail = base[:, span - 2 * LANES :]
            for r in range(rows // STEP):
                low = slice(r * STEP, (r + 1) * STEP)
                if r * STEP < half:
                    turned = base if r == 0 else pltpu.roll(base, r * STEP, 1)
                    at_row = pl.multiple_of((ct * per_tile + g) * half + r * STEP, STEP)
                    taps[pl.ds(at_row, STEP), :] = turned[:, :MAXDOC]
                    near = turned[:, MAXDOC:]
                else:
                    near = pltpu.roll(tail, r * STEP, 1)[:, LANES:]
                near_w[g * rows + r * STEP : g * rows + (r + 1) * STEP, :] = near * near_mask[low, :]
        block = own[j, :, pl.ds(pl.multiple_of(tile * LANES, LANES), LANES)]
        result = jnp.dot(near_w[...], block, preferred_element_type=f32)
        acc[ct] = pick(result, rows, slice(0, LANES))

    leader = jnp.broadcast_to(doc_row[0:1, 0:1], (rows, LANES))
    near_mask_out = (doc_col == leader).astype(f32)
    agree[0] = near_mask_out

    def far(j, tile):
        ct = j * tiles + tile
        lanes = slice(tile * LANES, (tile + 1) * LANES)
        pieces = []
        for w in range(REACH):
            q = lax.rem(at + w, REACH)
            slot = (q // 2 + at // 2) % 2 * 2 + (q + at) % 2
            pieces.append(got[slot, j, :, lanes] * far_mask[w])
        left = jnp.concatenate(pieces, 0)
        right = jnp.concatenate([left[half:], jnp.zeros((half, LANES), bf16)], 0)
        base = pl.multiple_of(ct * per_tile * half, per_tile * half)
        result = jnp.dot(
            taps[pl.ds(base, per_tile * half), :],
            jnp.concatenate([left, right], 1),
            preferred_element_type=f32,
        )
        both = jnp.concatenate(
            [pick(result, half, slice(0, LANES)), pick(result, half, slice(LANES, 2 * LANES))], 0
        )
        total = acc[ct] + both * agree[0]
        wide = pl.ds(pl.multiple_of(ct * LANES, LANES), LANES)
        out_ref[:, wide] = (gl_ref[:, wide].astype(f32) * total).astype(bf16)

    def step(s, _):
        @pl.when(s < CHUNKS)
        def _():
            lax.fori_loop(0, tiles, lambda tile, c: (prepare(s, tile), c)[1], 0)
            pl.when(has_prev)(lambda: await_recv(0, s))
            pl.when(upper == 1)(lambda: start(2, s, 0, row_mate))
            pl.when(core == 1)(lambda: start(1, s, 0, core_mate))

        @pl.when((s >= 1) & (s < CHUNKS + 1))
        def _():
            await_recv(2, s - 1)
            start(3, s - 1, 2, core_mate)

        @pl.when(s >= 2)
        def _():
            j = s - 2
            await_recv(1, j)
            await_recv(3, j)

            @pl.when(j == 0)
            def _():
                for w in range(REACH):
                    q = lax.rem(at + w, REACH)
                    slot = (q // 2 + at // 2) % 2 * 2 + (q + at) % 2
                    far_mask[w] = (got_doc[slot].astype(f32) == leader).astype(bf16)

            for tile in range(tiles):
                far(j, tile)

        return 0

    lax.fori_loop(0, CHUNKS + 2, step, 0)

    def drain(j, _):
        pl.when(has_next)(lambda: await_send(0, j))
        for slot in (1, 2, 3):
            await_send(slot, j)
        return 0

    lax.fori_loop(0, CHUNKS, drain, 0)
    pl.when(me < count - 1)(lambda: rim_copy(core_mate).wait_send())


def body(gate_short, key_short, value_short, gate_long, doc_ids, se_filter, long_filter):
    rows, chans = gate_short.shape
    tap_count, filters = se_filter.shape
    fgroup = chans // filters
    count = lax.axis_size("ctx")
    assert rows * REACH == MAXDOC and rows == LANES and count % REACH == 0
    width = chans // CHUNKS
    bf16, f32 = jnp.bfloat16, jnp.float32
    vmem = pl.BlockSpec(memory_space=pltpu.VMEM)
    return pl.pallas_call(
        functools.partial(kernel, count),
        out_shape=jax.ShapeDtypeStruct((rows, chans), bf16),
        in_specs=[vmem] * 7,
        out_specs=vmem,
        scratch_shapes=[
            pltpu.VMEM((CHUNKS, rows, width), bf16),
            pltpu.VMEM((rows, LANES), bf16),
            pltpu.VMEM((RIM, chans + LANES), bf16),
            pltpu.VMEM((RIM, chans + LANES), bf16),
            pltpu.VMEM((REACH, CHUNKS, rows, width), bf16),
            pltpu.VMEM((REACH, rows, LANES), bf16),
            pltpu.VMEM((filters * rows // 2, MAXDOC), bf16),
            pltpu.VMEM((filters, MAXDOC + rows), f32),
            pltpu.VMEM((LANES // fgroup * rows, rows), bf16),
            pltpu.VMEM((chans // LANES, rows, LANES), f32),
            pltpu.VMEM((tap_count, rows, LANES), f32),
            pltpu.VMEM((REACH, rows, LANES), bf16),
            pltpu.VMEM((rows, rows), bf16),
            pltpu.SemaphoreType.DMA((REACH, CHUNKS)),
            pltpu.SemaphoreType.DMA((REACH, CHUNKS)),
            pltpu.SemaphoreType.DMA((REACH,)),
            pltpu.SemaphoreType.DMA((REACH,)),
            pltpu.SemaphoreType.DMA,
            pltpu.SemaphoreType.DMA,
        ],
        compiler_params=pltpu.CompilerParams(
            collective_id=0, has_side_effects=True, vmem_limit_bytes=56 * 1024 * 1024
        ),
    )(gate_short, key_short, value_short, gate_long, doc_ids.reshape(1, rows), se_filter, long_filter)


def solution(mesh):
    placed = P(("groups", "ctx"), None)
    return jax.shard_map(
        body,
        mesh=mesh,
        in_specs=(placed, placed, placed, placed, P(("groups", "ctx")), P(), P()),
        out_specs=placed,
        check_vma=False,
    )
```

```python
import functools

import jax
import jax.numpy as jnp
from jax import lax
from jax.experimental import pallas as pl
from jax.experimental.pallas import tpu as pltpu
from jax.sharding import PartitionSpec as P

MAXDOC = 512
REACH = 4
RIM = 16
STEP = 16
LAG = 2
LANES = 128
CHUNKS = 16
MESH = pl.DeviceIdType.MESH


def kernel(
    count, gs_ref, k_ref, v_ref, gl_ref, doc_ref, se_ref, h_ref, out_ref,
    own, own_doc, rim_out, rim_in, got, got_doc, taps, rev, near_w, acc, agree, far_mask, near_mask,
    send_sem, recv_sem, doc_send, doc_recv, rim_send, rim_recv,
):
    rows, chans = gs_ref.shape
    tap_count = se_ref.shape[0]
    filters = h_ref.shape[0]
    width = chans // CHUNKS
    tiles = width // LANES
    fgroup = chans // filters
    per_tile = LANES // fgroup
    half = rows // 2
    span = MAXDOC + rows
    f32, bf16 = jnp.float32, jnp.bfloat16

    me = lax.axis_index("ctx")
    at = lax.rem(me, REACH)
    core = lax.rem(me, 2)
    upper = at // 2
    core_mate = me + 1 - 2 * core
    row_mate = me + 2 - 4 * upper
    has_prev = me >= REACH
    has_next = me + REACH < count
    is_first = me == 0
    is_last = me == count - 1

    barrier = pltpu.get_barrier_semaphore()

    def greet(target):
        pl.semaphore_signal(barrier, inc=1, device_id={"ctx": target}, device_id_type=MESH)

    greet(core_mate)
    greet(row_mate)
    pl.when(has_prev)(lambda: greet(me - REACH))
    pl.when(has_next)(lambda: greet(me + REACH))
    pl.when(me > 0)(lambda: greet(me - 1))
    pl.when(me < count - 1)(lambda: greet(me + 1))

    doc_row = jnp.broadcast_to(doc_ref[...].astype(f32), (rows, rows))
    doc_col = doc_row.T
    near_mask[...] = (doc_row == doc_col).astype(bf16)
    own_doc[...] = doc_col.astype(bf16)
    kv_tail = k_ref[rows - RIM :, :].astype(f32) * v_ref[rows - RIM :, :].astype(f32)
    rim_out[:, :chans] = kv_tail.astype(bf16)
    rim_out[:, chans:] = doc_col[rows - RIM :, :].astype(bf16)

    peers = 2 + has_prev.astype(jnp.int32) + has_next.astype(jnp.int32)
    peers = peers + (me > 0).astype(jnp.int32) + (me < count - 1).astype(jnp.int32)
    pl.semaphore_wait(barrier, peers)

    def remote(src, dst, ssem, rsem, target):
        return pltpu.make_async_remote_copy(
            src_ref=src, dst_ref=dst, send_sem=ssem, recv_sem=rsem,
            device_id={"ctx": target}, device_id_type=MESH,
        )

    def rim_copy(target):
        return remote(rim_out, rim_in, rim_send, rim_recv, target)

    pl.when(me < count - 1)(lambda: rim_copy(me + 1).start())

    def block_copy(slot, j, src, target):
        return remote(src, got.at[slot, j], send_sem.at[slot, j], recv_sem.at[slot, j], target)

    def doc_copy(slot, src, target):
        return remote(src, got_doc.at[slot], doc_send.at[slot], doc_recv.at[slot], target)

    def start(slot, j, source, target):
        block, docs = (own.at[j], own_doc) if source is None else (got.at[source, j], got_doc.at[source])
        pl.when(j == 0)(lambda: doc_copy(slot, docs, target).start())
        block_copy(slot, j, block, target).start()

    def await_recv(slot, j):
        pl.when(j == 0)(lambda: doc_copy(slot, own_doc, core_mate).wait_recv())
        block_copy(slot, j, own.at[j], core_mate).wait_recv()

    def await_send(slot, j):
        pl.when(j == 0)(lambda: doc_copy(slot, own_doc, core_mate).wait_send())
        block_copy(slot, j, own.at[j], core_mate).wait_send()

    @pl.when(is_first)
    def _():
        rim_in[:, :chans] = jnp.zeros((RIM, chans), bf16)
        rim_in[:, chans:] = jnp.full((RIM, LANES), -1.0, bf16)

    @pl.when(me > 0)
    def _():
        rim_copy(core_mate).wait_recv()

    doc_ext = jnp.concatenate([rim_in[:, chans:].astype(f32), doc_col], 0)
    for tap in range(tap_count):
        agree[tap] = (doc_ext[RIM - tap : RIM - tap + rows] == doc_col).astype(f32)

    left_over, terms = se_ref[...], []
    for _ in range(3):
        term = left_over.astype(bf16).astype(f32)
        left_over = left_over - term
        terms += [term, jnp.zeros((8 - tap_count, filters), f32)]
    se_parts = jnp.concatenate(terms, 0).astype(bf16)

    def short_chunk(j, _):
        source = lax.broadcasted_iota(jnp.int32, (filters, width), 0)
        target = lax.broadcasted_iota(jnp.int32, (filters, width), 1) // fgroup
        spread = jnp.where(source - j * (width // fgroup) == target, 1.0, 0.0).astype(bf16)
        parts = jnp.dot(se_parts, spread, preferred_element_type=f32)
        widened = parts[0:tap_count] + parts[8 : 8 + tap_count] + parts[16 : 16 + tap_count]
        for tile in range(tiles):
            lanes = pl.ds(pl.multiple_of(j * width + tile * LANES, LANES), LANES)
            kv = (k_ref[:, lanes].astype(f32) * v_ref[:, lanes].astype(f32)).astype(bf16).astype(f32)
            ext = jnp.concatenate([rim_in[:, lanes].astype(f32), kv], 0)
            weights = widened[:, tile * LANES : (tile + 1) * LANES]
            total = kv * weights[0:1, :]
            for tap in range(1, tap_count):
                shifted = ext[RIM - tap : RIM - tap + rows]
                total = total + (shifted * agree[tap]) * weights[tap : tap + 1, :]
            mixed = gs_ref[:, lanes].astype(f32) * total
            own[j, :, tile * LANES : (tile + 1) * LANES] = mixed.astype(bf16)
        pl.when(has_next)(lambda: start(0, j, None, me + REACH))
        pl.when(upper == 0)(lambda: start(2, j, None, row_mate))
        pl.when(core == 0)(lambda: start(1, j, None, core_mate))
        return 0

    lax.fori_loop(0, CHUNKS, short_chunk, 0)

    @pl.when(jnp.logical_not(has_prev))
    def _():
        got[0] = jnp.zeros(got.shape[1:], bf16)
        got_doc[0] = jnp.full(got_doc.shape[1:], -1.0, bf16)

    for piece in range(span // LANES):
        lag = lax.broadcasted_iota(jnp.int32, (MAXDOC, LANES), 0)
        pos = lax.broadcasted_iota(jnp.int32, (MAXDOC, LANES), 1) + piece * LANES
        flip = jnp.where(lag + pos == MAXDOC, 1.0, 0.0).astype(bf16)
        rev[:, piece * LANES : (piece + 1) * LANES] = jnp.dot(
            h_ref[...], flip, preferred_element_type=f32
        )

    lane_group = lax.broadcasted_iota(jnp.int32, (1, LANES), 1) // fgroup

    def pick(result, height, lanes):
        picked = result[0:height, lanes]
        for g in range(1, per_tile):
            picked = jnp.where(lane_group == g, result[g * height : (g + 1) * height, lanes], picked)
        return picked

    def prepare(j, tile):
        ct = j * tiles + tile
        first = pl.multiple_of(ct * per_tile, per_tile)
        filt = rev[pl.ds(first, per_tile), :]
        for g in range(per_tile):
            line = jnp.broadcast_to(filt[g : g + 1, :], (STEP, span))
            base = pltpu.roll(line, 0, 1, stride=1, stride_axis=0).astype(bf16)
            tail = base[:, span - 2 * LANES :]
            for r in range(rows // STEP):
                low = slice(r * STEP, (r + 1) * STEP)
                if r * STEP < half:
                    turned = base if r == 0 else pltpu.roll(base, r * STEP, 1)
                    at_row = pl.multiple_of((ct * per_tile + g) * half + r * STEP, STEP)
                    taps[pl.ds(at_row, STEP), :] = turned[:, :MAXDOC]
                    near = turned[:, MAXDOC:]
                else:
                    near = pltpu.roll(tail, r * STEP, 1)[:, LANES:]
                near_w[g * rows + r * STEP : g * rows + (r + 1) * STEP, :] = near * near_mask[low, :]
        block = own[j, :, pl.ds(pl.multiple_of(tile * LANES, LANES), LANES)]
        result = jnp.dot(near_w[...], block, preferred_element_type=f32)
        acc[ct] = pick(result, rows, slice(0, LANES))

    leader = jnp.broadcast_to(doc_row[0:1, 0:1], (rows, LANES))
    near_mask_out = (doc_col == leader).astype(f32)
    agree[0] = near_mask_out

    def far(j, tile):
        ct = j * tiles + tile
        lanes = slice(tile * LANES, (tile + 1) * LANES)
        pieces = []
        for w in range(REACH):
            q = lax.rem(at + w, REACH)
            slot = (q // 2 + at // 2) % 2 * 2 + (q + at) % 2
            pieces.append(got[slot, j, :, lanes] * far_mask[w])
        left = jnp.concatenate(pieces, 0)
        right = jnp.concatenate([left[half:], jnp.zeros((half, LANES), bf16)], 0)
        base = pl.multiple_of(ct * per_tile * half, per_tile * half)
        result = jnp.dot(
            taps[pl.ds(base, per_tile * half), :],
            jnp.concatenate([left, right], 1),
            preferred_element_type=f32,
        )
        both = jnp.concatenate(
            [pick(result, half, slice(0, LANES)), pick(result, half, slice(LANES, 2 * LANES))], 0
        )
        total = acc[ct] + both * agree[0]
        wide = pl.ds(pl.multiple_of(ct * LANES, LANES), LANES)
        out_ref[:, wide] = (gl_ref[:, wide].astype(f32) * total).astype(bf16)

    def step(s, _):
        @pl.when(s < CHUNKS)
        def _():
            lax.fori_loop(0, tiles, lambda tile, c: (prepare(s, tile), c)[1], 0)
            pl.when(has_prev)(lambda: await_recv(0, s))
            pl.when(upper == 1)(lambda: start(2, s, 0, row_mate))
            pl.when(core == 1)(lambda: start(1, s, 0, core_mate))

        @pl.when((s >= LAG) & (s < CHUNKS + LAG))
        def _():
            await_recv(2, s - LAG)
            start(3, s - LAG, 2, core_mate)

        @pl.when(s >= 2 * LAG)
        def _():
            j = s - 2 * LAG
            await_recv(1, j)
            await_recv(3, j)

            @pl.when(j == 0)
            def _():
                for w in range(REACH):
                    q = lax.rem(at + w, REACH)
                    slot = (q // 2 + at // 2) % 2 * 2 + (q + at) % 2
                    far_mask[w] = (got_doc[slot].astype(f32) == leader).astype(bf16)

            for tile in range(tiles):
                far(j, tile)

        return 0

    lax.fori_loop(0, CHUNKS + 2 * LAG, step, 0)

    def drain(j, _):
        pl.when(has_next)(lambda: await_send(0, j))
        for slot in (1, 2, 3):
            await_send(slot, j)
        return 0

    lax.fori_loop(0, CHUNKS, drain, 0)
    pl.when(me < count - 1)(lambda: rim_copy(core_mate).wait_send())


def body(gate_short, key_short, value_short, gate_long, doc_ids, se_filter, long_filter):
    rows, chans = gate_short.shape
    tap_count, filters = se_filter.shape
    fgroup = chans // filters
    count = lax.axis_size("ctx")
    assert rows * REACH == MAXDOC and rows == LANES and count % REACH == 0
    width = chans // CHUNKS
    bf16, f32 = jnp.bfloat16, jnp.float32
    vmem = pl.BlockSpec(memory_space=pltpu.VMEM)
    return pl.pallas_call(
        functools.partial(kernel, count),
        out_shape=jax.ShapeDtypeStruct((rows, chans), bf16),
        in_specs=[vmem] * 7,
        out_specs=vmem,
        scratch_shapes=[
            pltpu.VMEM((CHUNKS, rows, width), bf16),
            pltpu.VMEM((rows, LANES), bf16),
            pltpu.VMEM((RIM, chans + LANES), bf16),
            pltpu.VMEM((RIM, chans + LANES), bf16),
            pltpu.VMEM((REACH, CHUNKS, rows, width), bf16),
            pltpu.VMEM((REACH, rows, LANES), bf16),
            pltpu.VMEM((filters * rows // 2, MAXDOC), bf16),
            pltpu.VMEM((filters, MAXDOC + rows), f32),
            pltpu.VMEM((LANES // fgroup * rows, rows), bf16),
            pltpu.VMEM((chans // LANES, rows, LANES), f32),
            pltpu.VMEM((tap_count, rows, LANES), f32),
            pltpu.VMEM((REACH, rows, LANES), bf16),
            pltpu.VMEM((rows, rows), bf16),
            pltpu.SemaphoreType.DMA((REACH, CHUNKS)),
            pltpu.SemaphoreType.DMA((REACH, CHUNKS)),
            pltpu.SemaphoreType.DMA((REACH,)),
            pltpu.SemaphoreType.DMA((REACH,)),
            pltpu.SemaphoreType.DMA,
            pltpu.SemaphoreType.DMA,
        ],
        compiler_params=pltpu.CompilerParams(
            collective_id=0, has_side_effects=True, vmem_limit_bytes=56 * 1024 * 1024
        ),
    )(gate_short, key_short, value_short, gate_long, doc_ids.reshape(1, rows), se_filter, long_filter)


def solution(mesh):
    placed = P(("groups", "ctx"), None)
    return jax.shard_map(
        body,
        mesh=mesh,
        in_specs=(placed, placed, placed, placed, P(("groups", "ctx")), P(), P()),
        out_specs=placed,
        check_vma=False,
    )
```

```python
import functools

import jax
import jax.numpy as jnp
from jax import lax
from jax.experimental import pallas as pl
from jax.experimental.pallas import tpu as pltpu
from jax.sharding import PartitionSpec as P

MAXDOC = 512
REACH = 4
RIM = 16
STEP = 16
LAG = 1
LANES = 128
CHUNKS = 8
MESH = pl.DeviceIdType.MESH


def kernel(
    count, gs_ref, k_ref, v_ref, gl_ref, doc_ref, se_ref, h_ref, out_ref,
    own, own_doc, rim_out, rim_in, got, got_doc, taps, rev, near_w, acc, agree, far_mask, near_mask,
    send_sem, recv_sem, doc_send, doc_recv, rim_send, rim_recv,
):
    rows, chans = gs_ref.shape
    tap_count = se_ref.shape[0]
    filters = h_ref.shape[0]
    width = chans // CHUNKS
    tiles = width // LANES
    fgroup = chans // filters
    per_tile = LANES // fgroup
    half = rows // 2
    span = MAXDOC + rows
    f32, bf16 = jnp.float32, jnp.bfloat16

    me = lax.axis_index("ctx")
    at = lax.rem(me, REACH)
    core = lax.rem(me, 2)
    upper = at // 2
    core_mate = me + 1 - 2 * core
    row_mate = me + 2 - 4 * upper
    has_prev = me >= REACH
    has_next = me + REACH < count
    is_first = me == 0
    is_last = me == count - 1

    barrier = pltpu.get_barrier_semaphore()

    def greet(target):
        pl.semaphore_signal(barrier, inc=1, device_id={"ctx": target}, device_id_type=MESH)

    greet(core_mate)
    greet(row_mate)
    pl.when(has_prev)(lambda: greet(me - REACH))
    pl.when(has_next)(lambda: greet(me + REACH))
    pl.when(me > 0)(lambda: greet(me - 1))
    pl.when(me < count - 1)(lambda: greet(me + 1))

    doc_row = jnp.broadcast_to(doc_ref[...].astype(f32), (rows, rows))
    doc_col = doc_row.T
    near_mask[...] = (doc_row == doc_col).astype(bf16)
    own_doc[...] = doc_col.astype(bf16)
    kv_tail = k_ref[rows - RIM :, :].astype(f32) * v_ref[rows - RIM :, :].astype(f32)
    rim_out[:, :chans] = kv_tail.astype(bf16)
    rim_out[:, chans:] = doc_col[rows - RIM :, :].astype(bf16)

    peers = 2 + has_prev.astype(jnp.int32) + has_next.astype(jnp.int32)
    peers = peers + (me > 0).astype(jnp.int32) + (me < count - 1).astype(jnp.int32)
    pl.semaphore_wait(barrier, peers)

    def remote(src, dst, ssem, rsem, target):
        return pltpu.make_async_remote_copy(
            src_ref=src, dst_ref=dst, send_sem=ssem, recv_sem=rsem,
            device_id={"ctx": target}, device_id_type=MESH,
        )

    def rim_copy(target):
        return remote(rim_out, rim_in, rim_send, rim_recv, target)

    pl.when(me < count - 1)(lambda: rim_copy(me + 1).start())

    def block_copy(slot, j, src, target):
        return remote(src, got.at[slot, j], send_sem.at[slot, j], recv_sem.at[slot, j], target)

    def doc_copy(slot, src, target):
        return remote(src, got_doc.at[slot], doc_send.at[slot], doc_recv.at[slot], target)

    def start(slot, j, source, target):
        block, docs = (own.at[j], own_doc) if source is None else (got.at[source, j], got_doc.at[source])
        pl.when(j == 0)(lambda: doc_copy(slot, docs, target).start())
        block_copy(slot, j, block, target).start()

    def await_recv(slot, j):
        pl.when(j == 0)(lambda: doc_copy(slot, own_doc, core_mate).wait_recv())
        block_copy(slot, j, own.at[j], core_mate).wait_recv()

    def await_send(slot, j):
        pl.when(j == 0)(lambda: doc_copy(slot, own_doc, core_mate).wait_send())
        block_copy(slot, j, own.at[j], core_mate).wait_send()

    @pl.when(is_first)
    def _():
        rim_in[:, :chans] = jnp.zeros((RIM, chans), bf16)
        rim_in[:, chans:] = jnp.full((RIM, LANES), -1.0, bf16)

    @pl.when(me > 0)
    def _():
        rim_copy(core_mate).wait_recv()

    doc_ext = jnp.concatenate([rim_in[:, chans:].astype(f32), doc_col], 0)
    for tap in range(tap_count):
        agree[tap] = (doc_ext[RIM - tap : RIM - tap + rows] == doc_col).astype(f32)

    left_over, terms = se_ref[...], []
    for _ in range(3):
        term = left_over.astype(bf16).astype(f32)
        left_over = left_over - term
        terms += [term, jnp.zeros((8 - tap_count, filters), f32)]
    se_parts = jnp.concatenate(terms, 0).astype(bf16)

    def short_chunk(j, _):
        source = lax.broadcasted_iota(jnp.int32, (filters, width), 0)
        target = lax.broadcasted_iota(jnp.int32, (filters, width), 1) // fgroup
        spread = jnp.where(source - j * (width // fgroup) == target, 1.0, 0.0).astype(bf16)
        parts = jnp.dot(se_parts, spread, preferred_element_type=f32)
        widened = parts[0:tap_count] + parts[8 : 8 + tap_count] + parts[16 : 16 + tap_count]
        for tile in range(tiles):
            lanes = pl.ds(pl.multiple_of(j * width + tile * LANES, LANES), LANES)
            kv = (k_ref[:, lanes].astype(f32) * v_ref[:, lanes].astype(f32)).astype(bf16).astype(f32)
            ext = jnp.concatenate([rim_in[:, lanes].astype(f32), kv], 0)
            weights = widened[:, tile * LANES : (tile + 1) * LANES]
            total = kv * weights[0:1, :]
            for tap in range(1, tap_count):
                shifted = ext[RIM - tap : RIM - tap + rows]
                total = total + (shifted * agree[tap]) * weights[tap : tap + 1, :]
            mixed = gs_ref[:, lanes].astype(f32) * total
            own[j, :, tile * LANES : (tile + 1) * LANES] = mixed.astype(bf16)
        pl.when(has_next)(lambda: start(0, j, None, me + REACH))
        pl.when(upper == 0)(lambda: start(2, j, None, row_mate))
        pl.when(core == 0)(lambda: start(1, j, None, core_mate))
        return 0

    lax.fori_loop(0, CHUNKS, short_chunk, 0)

    @pl.when(jnp.logical_not(has_prev))
    def _():
        got[0] = jnp.zeros(got.shape[1:], bf16)
        got_doc[0] = jnp.full(got_doc.shape[1:], -1.0, bf16)

    for piece in range(span // LANES):
        lag = lax.broadcasted_iota(jnp.int32, (MAXDOC, LANES), 0)
        pos = lax.broadcasted_iota(jnp.int32, (MAXDOC, LANES), 1) + piece * LANES
        flip = jnp.where(lag + pos == MAXDOC, 1.0, 0.0).astype(bf16)
        rev[:, piece * LANES : (piece + 1) * LANES] = jnp.dot(
            h_ref[...], flip, preferred_element_type=f32
        )

    lane_group = lax.broadcasted_iota(jnp.int32, (1, LANES), 1) // fgroup

    def pick(result, height, lanes):
        picked = result[0:height, lanes]
        for g in range(1, per_tile):
            picked = jnp.where(lane_group == g, result[g * height : (g + 1) * height, lanes], picked)
        return picked

    def prepare(j, tile):
        ct = j * tiles + tile
        first = pl.multiple_of(ct * per_tile, per_tile)
        filt = rev[pl.ds(first, per_tile), :]
        for g in range(per_tile):
            line = jnp.broadcast_to(filt[g : g + 1, :], (STEP, span))
            base = pltpu.roll(line, 0, 1, stride=1, stride_axis=0).astype(bf16)
            tail = base[:, span - 2 * LANES :]
            for r in range(rows // STEP):
                low = slice(r * STEP, (r + 1) * STEP)
                if r * STEP < half:
                    turned = base if r == 0 else pltpu.roll(base, r * STEP, 1)
                    at_row = pl.multiple_of((ct * per_tile + g) * half + r * STEP, STEP)
                    taps[pl.ds(at_row, STEP), :] = turned[:, :MAXDOC]
                    near = turned[:, MAXDOC:]
                else:
                    near = pltpu.roll(tail, r * STEP, 1)[:, LANES:]
                near_w[g * rows + r * STEP : g * rows + (r + 1) * STEP, :] = near * near_mask[low, :]
        block = own[j, :, pl.ds(pl.multiple_of(tile * LANES, LANES), LANES)]
        result = jnp.dot(near_w[...], block, preferred_element_type=f32)
        acc[ct] = pick(result, rows, slice(0, LANES))

    leader = jnp.broadcast_to(doc_row[0:1, 0:1], (rows, LANES))
    near_mask_out = (doc_col == leader).astype(f32)
    agree[0] = near_mask_out

    def far(j, tile):
        ct = j * tiles + tile
        lanes = slice(tile * LANES, (tile + 1) * LANES)
        pieces = []
        for w in range(REACH):
            q = lax.rem(at + w, REACH)
            slot = (q // 2 + at // 2) % 2 * 2 + (q + at) % 2
            pieces.append(got[slot, j, :, lanes] * far_mask[w])
        left = jnp.concatenate(pieces, 0)
        right = jnp.concatenate([left[half:], jnp.zeros((half, LANES), bf16)], 0)
        base = pl.multiple_of(ct * per_tile * half, per_tile * half)
        result = jnp.dot(
            taps[pl.ds(base, per_tile * half), :],
            jnp.concatenate([left, right], 1),
            preferred_element_type=f32,
        )
        both = jnp.concatenate(
            [pick(result, half, slice(0, LANES)), pick(result, half, slice(LANES, 2 * LANES))], 0
        )
        total = acc[ct] + both * agree[0]
        wide = pl.ds(pl.multiple_of(ct * LANES, LANES), LANES)
        out_ref[:, wide] = (gl_ref[:, wide].astype(f32) * total).astype(bf16)

    def step(s, _):
        @pl.when(s < CHUNKS)
        def _():
            lax.fori_loop(0, tiles, lambda tile, c: (prepare(s, tile), c)[1], 0)
            pl.when(has_prev)(lambda: await_recv(0, s))
            pl.when(upper == 1)(lambda: start(2, s, 0, row_mate))
            pl.when(core == 1)(lambda: start(1, s, 0, core_mate))

        @pl.when((s >= LAG) & (s < CHUNKS + LAG))
        def _():
            await_recv(2, s - LAG)
            start(3, s - LAG, 2, core_mate)

        @pl.when(s >= 2 * LAG)
        def _():
            j = s - 2 * LAG
            await_recv(1, j)
            await_recv(3, j)

            @pl.when(j == 0)
            def _():
                for w in range(REACH):
                    q = lax.rem(at + w, REACH)
                    slot = (q // 2 + at // 2) % 2 * 2 + (q + at) % 2
                    far_mask[w] = (got_doc[slot].astype(f32) == leader).astype(bf16)

            for tile in range(tiles):
                far(j, tile)

        return 0

    lax.fori_loop(0, CHUNKS + 2 * LAG, step, 0)

    def drain(j, _):
        pl.when(has_next)(lambda: await_send(0, j))
        for slot in (1, 2, 3):
            await_send(slot, j)
        return 0

    lax.fori_loop(0, CHUNKS, drain, 0)
    pl.when(me < count - 1)(lambda: rim_copy(core_mate).wait_send())


def body(gate_short, key_short, value_short, gate_long, doc_ids, se_filter, long_filter):
    rows, chans = gate_short.shape
    tap_count, filters = se_filter.shape
    fgroup = chans // filters
    count = lax.axis_size("ctx")
    assert rows * REACH == MAXDOC and rows == LANES and count % REACH == 0
    width = chans // CHUNKS
    bf16, f32 = jnp.bfloat16, jnp.float32
    vmem = pl.BlockSpec(memory_space=pltpu.VMEM)
    return pl.pallas_call(
        functools.partial(kernel, count),
        out_shape=jax.ShapeDtypeStruct((rows, chans), bf16),
        in_specs=[vmem] * 7,
        out_specs=vmem,
        scratch_shapes=[
            pltpu.VMEM((CHUNKS, rows, width), bf16),
            pltpu.VMEM((rows, LANES), bf16),
            pltpu.VMEM((RIM, chans + LANES), bf16),
            pltpu.VMEM((RIM, chans + LANES), bf16),
            pltpu.VMEM((REACH, CHUNKS, rows, width), bf16),
            pltpu.VMEM((REACH, rows, LANES), bf16),
            pltpu.VMEM((filters * rows // 2, MAXDOC), bf16),
            pltpu.VMEM((filters, MAXDOC + rows), f32),
            pltpu.VMEM((LANES // fgroup * rows, rows), bf16),
            pltpu.VMEM((chans // LANES, rows, LANES), f32),
            pltpu.VMEM((tap_count, rows, LANES), f32),
            pltpu.VMEM((REACH, rows, LANES), bf16),
            pltpu.VMEM((rows, rows), bf16),
            pltpu.SemaphoreType.DMA((REACH, CHUNKS)),
            pltpu.SemaphoreType.DMA((REACH, CHUNKS)),
            pltpu.SemaphoreType.DMA((REACH,)),
            pltpu.SemaphoreType.DMA((REACH,)),
            pltpu.SemaphoreType.DMA,
            pltpu.SemaphoreType.DMA,
        ],
        compiler_params=pltpu.CompilerParams(
            collective_id=0, has_side_effects=True, vmem_limit_bytes=56 * 1024 * 1024
        ),
    )(gate_short, key_short, value_short, gate_long, doc_ids.reshape(1, rows), se_filter, long_filter)


def solution(mesh):
    placed = P(("groups", "ctx"), None)
    return jax.shard_map(
        body,
        mesh=mesh,
        in_specs=(placed, placed, placed, placed, P(("groups", "ctx")), P(), P()),
        out_specs=placed,
        check_vma=False,
    )
```
